32 devices in a mesh: sub: 4 (over z), crow: 2 (over x), ccol: 4 (over y, core).
Axes of the slice: x: 2, y: 2, z: 4, core: 2. Of those that a mesh axis runs over, the one named last changes fastest.
Arguments:
- right_side: bfloat16 [32, 1536, 128], P(('sub', 'crow', 'ccol')), may hold values from -6 to 6
- stiff_diag: float32 [32, 1536], P(('sub', 'crow', 'ccol')), may hold values from 1 to 4
- dual_op: bfloat16 [32, 1536, 1536], P(('sub', 'crow', 'ccol')), may hold values from -0.15625 to 0.15625
- schur_op: bfloat16 [32, 1536, 1536], P(('sub', 'crow', 'ccol')), may hold values from -0.15625 to 0.15625
- modes: bfloat16 [32, 1536, 64], P(('sub', 'crow', 'ccol')), may hold values from -0.15625 to 0.15625
- coarse_inverse: bfloat16 [8, 4, 64, 8, 256], P(None, 'sub', None, ('crow', 'ccol')), may hold values from -0.125 to 0.125
- face_index: int32 [32, 2, 384], replicated, may hold values from 0 to 1535, as said below
Outputs:
- multipliers: float32 [32, 1536, 128], P(('sub', 'crow', 'ccol'))
- residual: bfloat16 [32, 1536, 128], P(('sub', 'crow', 'ccol'))
The draws below stay inside these ranges and needn't reach their ends.
Inputs may be any that keep to these rules, and one draw needn't show every extreme that they name: `face_index`: for each subdomain its 768 entries are distinct.
All inputs are finite; a program needn't handle non-finite values.
Results may differ from the reference program's by a relative error of at most 0.0055.
Values may be sent and summed in bfloat16 or wider, within the bound.
A program may use at most 64 MiB of HBM per device.

```python
import math
import jax
import jax.numpy as jnp
from jax import lax

M = 1536
MODES = 64
LOADS = 128
FACE = 384
CHAIN = 4
GROUPS = 8
SUBS = 32
COARSE = 2048


def draw_face_index(key, part):
    keys = jax.random.split(jax.random.fold_in(key, 17), SUBS)

    def one_subdomain(sub_key):
        return jax.random.permutation(sub_key, M)[:2 * FACE].reshape(2, FACE)
    return jax.vmap(one_subdomain)(keys).astype(jnp.int32)


def steps_of(key, extent, shards, low, high):
    def one(dim, parts):
        draws = jax.random.uniform(jax.random.fold_in(jax.random.fold_in(key, 6), dim), (parts,), jnp.float32, low / len(shards), high / len(shards))
        return jnp.repeat(jnp.exp(draws), extent[dim] // parts).reshape((-1,) + (1,) * (len(extent) - dim - 1))

    factor_of = one(*shards[0])
    for cut in shards[1:]:
        factor_of = factor_of * one(*cut)
    return factor_of


def scatter_about(key, dims, spread, reach, shards=(), dtype=jnp.bfloat16):
    factor_of = steps_of(key, dims, shards, -0.22, 0.18) if shards else 1.0
    values = jax.random.normal(key, dims, jnp.float32) * spread * factor_of
    return jnp.minimum(jnp.maximum(values, -reach), reach).astype(dtype)


def setup_inputs(seed: int = 0) -> dict:
    streams_of = jax.random.split(jax.random.key(seed), 8)
    return {
        "right_side": scatter_about(streams_of[0], (SUBS, M, LOADS), 1.0, 6.0, ((0, 32),)),
        "stiff_diag": jnp.clip(jnp.exp(math.log(4.0) - 1.3862944 * jax.random.uniform(streams_of[1], (SUBS, M), jnp.float32) ** steps_of(streams_of[1], (SUBS, M), ((0, 32),), -0.2, 0.2)), 1.0, 4.0),
        "dual_op": scatter_about(streams_of[2], (SUBS, M, M), M ** -0.5, 0.15625, ((0, 32),)),
        "schur_op": scatter_about(streams_of[3], (SUBS, M, M), M ** -0.5, 0.15625, ((0, 32),)),
        "modes": scatter_about(streams_of[4], (SUBS, M, MODES), M ** -0.5, 0.15625, ((0, 32),)),
        "coarse_inverse": scatter_about(streams_of[5], (GROUPS, CHAIN, MODES, GROUPS, CHAIN * MODES), COARSE ** -0.5, 0.125, ((1, 4), (3, 8))),
        "face_index": draw_face_index(jax.random.fold_in(streams_of[7], 71), 0),
    }


spectrum_low = 0.5
spectrum_high = 4.0


def batched_dot(left, right):
    return lax.map(lambda pair: jnp.dot(pair[0], pair[1], preferred_element_type=jnp.float32), (left, right))


def dual_apply(vector, stiff_diag, dual_op, face_index):
    product = batched_dot(dual_op, vector.astype(jnp.bfloat16))
    lower_rows = face_index[:, 0, :]
    upper_rows = face_index[:, 1, :]
    picker = jax.vmap(lambda values, rows: values[rows])
    upper_vals = picker(product, upper_rows).reshape(CHAIN, GROUPS, FACE, LOADS)
    lower_vals = picker(product, lower_rows).reshape(CHAIN, GROUPS, FACE, LOADS)
    blank = jnp.zeros((1, GROUPS, FACE, LOADS), jnp.float32)
    from_prev = jnp.concatenate([blank, upper_vals[:-1]], 0).reshape(SUBS, FACE, LOADS)
    from_next = jnp.concatenate([lower_vals[1:], blank], 0).reshape(SUBS, FACE, LOADS)
    result = stiff_diag[:, :, None] * vector + product
    adder = jax.vmap(lambda values, rows, extra: values.at[rows].add(-extra))
    result = adder(result, lower_rows, from_prev)
    result = adder(result, upper_rows, from_next)
    return result


def precondition(residual, schur_op, modes, coarse_inverse):
    rounded = residual.astype(jnp.bfloat16)
    smooth = batched_dot(schur_op, rounded)
    coeff = lax.map(lambda pair: jnp.dot(pair[0].T, pair[1], preferred_element_type=jnp.float32), (modes, rounded)).astype(jnp.bfloat16)
    ordered = coeff.reshape(CHAIN, GROUPS, MODES, LOADS).transpose(1, 0, 2, 3).reshape(COARSE, LOADS)
    matrix = coarse_inverse.reshape(COARSE, COARSE)
    solved = jnp.dot(matrix, ordered, preferred_element_type=jnp.float32).astype(jnp.bfloat16)
    back = solved.reshape(GROUPS, CHAIN, MODES, LOADS).transpose(1, 0, 2, 3).reshape(SUBS, MODES, LOADS)
    return smooth + batched_dot(modes, back)


def reference(right_side, stiff_diag, dual_op, schur_op, modes, coarse_inverse, face_index):
    center = (spectrum_high + spectrum_low) / 2.0
    half_width = (spectrum_high - spectrum_low) / 2.0
    first_res = right_side.astype(jnp.float32)
    first_step = precondition(first_res, schur_op, modes, coarse_inverse) / center
    multipliers = first_step
    second_res = first_res - dual_apply(first_step, stiff_diag, dual_op, face_index)
    ratio_old = half_width / center
    ratio_new = 1.0 / (2.0 * center / half_width - ratio_old)
    second_step = ratio_new * ratio_old * first_step + (2.0 * ratio_new / half_width) * precondition(second_res, schur_op, modes, coarse_inverse)
    multipliers = multipliers + second_step
    final_res = second_res - dual_apply(second_step, stiff_diag, dual_op, face_index)
    return multipliers, final_res.astype(jnp.bfloat16)
```

```python
import functools

import jax
import jax.numpy as jnp
from jax import lax
from jax.experimental import pallas as pl
from jax.experimental.pallas import tpu as pltpu
from jax.sharding import PartitionSpec as P

spectrum_low = 0.5
spectrum_high = 4.0
center = (spectrum_high + spectrum_low) / 2.0
half_width = (spectrum_high - spectrum_low) / 2.0
ratio_old = half_width / center
ratio_new = 1.0 / (2.0 * center / half_width - ratio_old)
carry = ratio_new * ratio_old
gain = 2.0 * ratio_new / half_width

F32 = jnp.float32
BF16 = jnp.bfloat16
MESH = pl.DeviceIdType.MESH


def mm(left, right):
    return jnp.dot(left, right, preferred_element_type=F32)


def kernel(
    dims,
    rhs_h, diag_h, dual_h, schur_h, modes_h, coarse_h, face_h,
    mult, res,
    rhs, diag, dual, schur, modes_t, modes, coarse, face,
    rows_of, pick, put, vec, work, base, step0, prod, own, gh, kf, yz, bfull, cvec,
    ag0, agc, aga, bc, part, rs, solved, near, mft, mrecv, ysend, yrecv, zsend, zrecv,
    in_sem, sch_sem, dua_sem, ag_s, ag_r, rs_s, rs_r, nb_s, nb_r, hm_s, hm_r,
    hy_s, hy_r, hz_s, hz_r,
):
    subs, crows, ccols = dims
    groups = crows * ccols
    m = rhs.shape[0]
    loads = rhs.shape[1]
    nm = modes.shape[1]
    face_n = face.shape[1]
    ch = 512 if m % 512 == 0 else m
    chunks = m // ch
    half = face_n // 2
    inv = 1.0 / center
    sub = lax.axis_index("sub")
    crow = lax.axis_index("crow")
    ccol = lax.axis_index("ccol")
    group = crow * ccols + ccol
    flat = sub * groups + group

    def local(src, dst, sem):
        return pltpu.make_async_copy(src, dst, sem)

    loads_in = [
        local(rhs_h.at[0], rhs, in_sem.at[0]),
        local(modes_h.at[0], modes_t, in_sem.at[1]),
        local(face_h.at[flat], face, in_sem.at[2]),
        local(diag_h, diag, in_sem.at[3]),
        local(coarse_h, coarse, in_sem.at[4]),
    ]
    sch_in = [
        local(schur_h.at[0, pl.ds(k * ch, ch)], schur.at[pl.ds(k * ch, ch)], sch_sem.at[k])
        for k in range(chunks)
    ]
    dua_in = [
        local(dual_h.at[0, pl.ds(k * ch, ch)], dual.at[pl.ds(k * ch, ch)], dua_sem.at[k])
        for k in range(chunks)
    ]
    for c in loads_in[:3] + sch_in + loads_in[3:]:
        c.start()

    def sub_id(s):
        return (s, crow, ccol)

    def group_id(g):
        return (sub, g // ccols, lax.rem(g, ccols))

    barrier = pltpu.get_barrier_semaphore()
    for d in range(1, subs):
        pl.semaphore_signal(
            barrier, inc=1, device_id=sub_id(lax.rem(sub + d, subs)), device_id_type=MESH
        )
    for d in range(1, groups):
        pl.semaphore_signal(
            barrier, inc=1, device_id=group_id(lax.rem(group + d, groups)), device_id_type=MESH
        )

    def remote(src, dst, s_sem, r_sem, dev):
        return pltpu.make_async_remote_copy(
            src_ref=src, dst_ref=dst, send_sem=s_sem, recv_sem=r_sem,
            device_id=dev, device_id_type=MESH,
        )

    def gather(i, buf):
        return [
            remote(buf.at[sub], buf.at[sub], ag_s.at[i, d - 1], ag_r.at[i, d - 1],
                   sub_id(lax.rem(sub + d, subs)))
            for d in range(1, subs)
        ]

    gather0, gather_c, gather_a, gather_b = (
        gather(i, buf) for i, buf in enumerate((ag0, agc, aga, bc))
    )
    far = [ccols // 2] + [c for c in range(1, ccols) if c != ccols // 2]
    hops = [(r, c) for r in range(1, crows) for c in far + [0]] + [(0, c) for c in far]
    scatters = []
    for t in range(2):
        row = []
        for d, (dr, dc) in enumerate(hops):
            r, c = lax.rem(crow + dr, crows), lax.rem(ccol + dc, ccols)
            row.append(
                remote(part.at[t, r * ccols + c], rs.at[t, d], rs_s.at[t, d], rs_r.at[t, d],
                       (sub, r, c))
            )
        scatters.append(row)
    has_next = sub < subs - 1
    has_prev = sub > 0
    after = sub_id(jnp.minimum(sub + 1, subs - 1))
    before = sub_id(jnp.maximum(sub - 1, 0))
    ends = ((0, 1, after, has_next, has_prev), (1, 0, before, has_prev, has_next))

    def near_copy(e):
        return remote(solved, near.at[e], nb_s.at[e], nb_r.at[e], ends[e][2])

    def m_copy(e):
        return remote(mft.at[ends[e][1]], mrecv.at[e], hm_s.at[e], hm_r.at[e], ends[e][2])

    def y_copy(t, e):
        return remote(ysend.at[t, ends[e][1]], yrecv.at[t, e], hy_s.at[t, e], hy_r.at[t, e],
                      ends[e][2])

    def z_copy(e):
        return remote(zsend.at[ends[e][1]], zrecv.at[e], hz_s.at[e], hz_r.at[e], ends[e][2])

    def send(make):
        for e in range(2):
            pl.when(ends[e][3])(lambda e=e: make(e).start())

    def arrive(make):
        for e in range(2):
            pl.when(ends[e][4])(lambda e=e: make(e).wait_recv())

    def drain(make):
        for e in range(2):
            pl.when(ends[e][3])(lambda e=e: make(e).wait_send())

    for e in range(2):

        @pl.when(jnp.logical_not(ends[e][4]))
        def _(e=e):
            zrecv[e] = jnp.zeros_like(zrecv[e])
            mrecv[e] = jnp.zeros_like(mrecv[e])
            near[e] = jnp.zeros_like(near[e])
            for t in range(2):
                yrecv[t, e] = jnp.zeros_like(yrecv[t, e])

    def rows(k):
        return pl.ds(k * ch, ch)

    loads_in[0].wait()
    loads_in[1].wait()
    ag0[sub] = mm(modes_t[...], rhs[...]).astype(BF16)
    pl.semaphore_wait(barrier, subs - 1 + groups - 1)
    for c in gather0:
        c.start()

    loads_in[2].wait()
    lane = lax.broadcasted_iota(jnp.int32, (face_n, 128), 1)
    for e in range(2):
        wide = jnp.broadcast_to(face[e:e + 1, :], (128, face_n)).T
        for c in range(m // 128):
            pick[e * face_n:(e + 1) * face_n, c * 128:(c + 1) * 128] = jnp.where(
                wide == lane + c * 128, 1.0, 0.0
            ).astype(BF16)
    modes[...] = modes_t[...].T
    vec[:, loads:loads + nm] = modes[...]
    for e in range(2):
        mft[e] = mm(pick[e * face_n:(e + 1) * face_n, :], modes[...]).astype(BF16).T
    send(m_copy)

    for k in range(chunks):
        sch_in[k].wait()
        dua_in[k].start()
    for k in range(chunks):
        u = mm(schur[rows(k), :], rhs[...]) * inv
        step0[rows(k), :] = u
        vec[rows(k), :loads] = u.astype(BF16)

    loads_in[3].wait()
    sub_row = lax.broadcasted_iota(jnp.int32, (128, face_n), 0)
    for c in range(m // 128):
        span = slice(c * 128, (c + 1) * 128)
        for e in range(2):
            put[span, e * face_n:(e + 1) * face_n] = jnp.where(
                face[e:e + 1, :] == sub_row + c * 128, 1.0, 0.0
            ).astype(BF16)
        rows_of[span, :] = jnp.broadcast_to(diag[:, span], (128, 128)).T
    bfull[...] = jnp.zeros_like(bfull)

    for c in dua_in:
        c.wait()
    for k in range(chunks):
        y = mm(dual[rows(k), :], vec[...])
        work[rows(k), :] = y.astype(BF16)
        b = rhs[rows(k), :].astype(F32) - rows_of[rows(k), :] * step0[rows(k), :] - y[:, :loads]
        base[rows(k), :] = b
        own[rows(k), :] = b.astype(BF16)
        gh[rows(k), 2 * nm:] = (
            rows_of[rows(k), :nm] * modes[rows(k), :].astype(F32) + y[:, loads:]
        ).astype(BF16)
    for e in range(2):
        got = mm(pick[e * face_n:(e + 1) * face_n, :], work[...])
        ysend[0, e] = got[:, :loads].astype(BF16)
        faces = got[:, loads:].astype(BF16)
        kf[e] = faces
        zsend[e] = jnp.concatenate([faces[:half], faces[half:]], axis=1)
    send(functools.partial(y_copy, 0))
    send(z_copy)

    def scatter(t, coeff):
        part[t] = mm(coarse[...], coeff).astype(BF16).reshape(groups, nm, loads)
        for c in scatters[t]:
            c.start()

    def total(t):
        out = part[t, group].astype(F32)
        for d in range(1, groups):
            scatters[t][d - 1].wait_recv()
            out = out + rs[t, d - 1].astype(F32)
        return out.astype(BF16)

    loads_in[4].wait()
    for c in gather0:
        c.wait_recv()
    scatter(0, ag0[...].reshape(subs * nm, loads))

    plain = mm(modes_t[...], own[...])
    arrive(m_copy)
    bc[sub] = jnp.concatenate(
        [
            mm(mrecv[0], kf[0]) * inv,
            mm(modes_t[...], gh[:, 2 * nm:]) * (-inv),
            mm(mrecv[1], kf[1]) * inv,
        ],
        axis=1,
    ).astype(BF16)
    for c in gather_b:
        c.start()

    agc[sub] = total(0)
    for c in gather_c:
        c.start()
    arrive(functools.partial(y_copy, 0))
    aga[sub] = (plain + mm(mft[0], yrecv[0, 0]) + mm(mft[1], yrecv[0, 1])).astype(BF16)
    for c in gather_a:
        c.start()

    arrive(z_copy)
    blank = jnp.zeros((face_n, nm), BF16)
    for e in range(2):
        span = slice(e * face_n, (e + 1) * face_n)
        yz[span, :loads] = yrecv[0, e]
        z = jnp.concatenate([zrecv[e, :, :nm], zrecv[e, :, nm:]], axis=0)
        yz[span, loads:] = jnp.concatenate([z, blank] if e == 0 else [blank, z], axis=1)
    for k in range(chunks):
        got = mm(put[rows(k), :], yz[...])
        base[rows(k), :] += got[:, :loads]
        gh[rows(k), :2 * nm] = got[:, loads:].astype(BF16)
    for k in range(chunks):
        step0[rows(k), :] += mm(modes[rows(k), :], agc[sub]) * inv

    first, last = gather_c[0], gather_c[-1]
    if subs > 2:
        pl.when(has_prev)(first.wait_recv)
        pl.when(has_next)(last.wait_recv)
    elif subs == 2:
        first.wait_recv()
    cvec[:nm] = agc[jnp.maximum(sub - 1, 0)]
    cvec[nm:2 * nm] = agc[jnp.minimum(sub + 1, subs - 1)]
    cvec[2 * nm:] = -agc[sub]
    for k in range(chunks):
        r1 = base[rows(k), :] + mm(gh[rows(k), :], cvec[...]) * inv
        base[rows(k), :] = r1
        own[rows(k), :] = r1.astype(BF16)
    for k in range(chunks):
        w = carry * step0[rows(k), :] + gain * mm(schur[rows(k), :], own[...])
        prod[rows(k), :] = w
        vec[rows(k), :loads] = w.astype(BF16)

    for c in gather_b:
        c.wait_recv()
    for t in range(subs):
        for j, s in enumerate((t - 1, t, t + 1)):
            if 0 <= s < subs:
                bfull[s * nm:(s + 1) * nm, t * nm:(t + 1) * nm] = bc[t, :, j * nm:(j + 1) * nm]
    if subs > 2:
        pl.when(jnp.logical_not(has_prev))(first.wait_recv)
        pl.when(jnp.logical_not(has_next))(last.wait_recv)
        for c in gather_c[1:-1]:
            c.wait_recv()
    for c in gather_a:
        c.wait_recv()
    coeff = aga[...].reshape(subs * nm, loads).astype(F32) + mm(
        bfull[...], agc[...].reshape(subs * nm, loads)
    )
    scatter(1, coeff.astype(BF16))

    for k in range(chunks):
        y = mm(dual[rows(k), :], vec[:, :loads])
        base[rows(k), :] = base[rows(k), :] - y - rows_of[rows(k), :] * prod[rows(k), :]
        own[rows(k), :] = y.astype(BF16)
    for e in range(2):
        ysend[1, e] = mm(pick[e * face_n:(e + 1) * face_n, :], own[...]).astype(BF16)
    send(functools.partial(y_copy, 1))

    solved[...] = total(1)
    send(near_copy)
    for k in range(chunks):
        mult[rows(k), :] = (
            step0[rows(k), :] + prod[rows(k), :] + gain * mm(modes[rows(k), :], solved[...])
        )
        base[rows(k), :] -= gain * mm(gh[rows(k), 2 * nm:], solved[...])
    arrive(functools.partial(y_copy, 1))
    for k in range(chunks):
        base[rows(k), :] += mm(put[rows(k), :], yrecv[1].reshape(2 * face_n, loads))
    arrive(near_copy)
    for k in range(chunks):
        res[rows(k), :] = (
            base[rows(k), :]
            + gain * mm(gh[rows(k), :2 * nm], near[...].reshape(2 * nm, loads))
        ).astype(BF16)
    for c in gather0 + gather_c + gather_a + gather_b + scatters[0] + scatters[1]:
        c.wait_send()
    for t in range(2):
        drain(functools.partial(y_copy, t))
    drain(near_copy)
    drain(m_copy)
    drain(z_copy)


def write_out(mult, res, mult_h, res_h, sem):
    copies = [
        pltpu.make_async_copy(mult, mult_h.at[0], sem.at[0]),
        pltpu.make_async_copy(res, res_h.at[0], sem.at[1]),
    ]
    for c in copies:
        c.start()
    for c in copies:
        c.wait()


def local(dims, right_side, stiff_diag, dual_op, schur_op, modes, coarse_inverse, face_index):
    subs, crows, ccols = dims
    groups = crows * ccols
    _, m, loads = right_side.shape
    nm = modes.shape[2]
    face_n = face_index.shape[2]
    coarse = coarse_inverse.reshape(
        coarse_inverse.shape[0] * coarse_inverse.shape[2], coarse_inverse.shape[4]
    )
    ch = 512 if m % 512 == 0 else m
    v = pltpu.VMEM
    dma = pltpu.SemaphoreType.DMA
    any_spec = pl.BlockSpec(memory_space=pl.ANY)
    mult, res = pl.pallas_call(
        functools.partial(kernel, dims),
        out_shape=(v((m, loads), F32), v((m, loads), BF16)),
        in_specs=[pl.BlockSpec(memory_space=pltpu.HBM)] * 7,
        out_specs=(pl.BlockSpec(memory_space=pltpu.VMEM),) * 2,
        scratch_shapes=[
            v((m, loads), BF16), v((1, m), F32), v((m, m), BF16), v((m, m), BF16),
            v((nm, m), BF16), v((m, nm), BF16), v(coarse.shape, BF16), v((2, face_n), jnp.int32),
            v((m, loads), F32), v((2 * face_n, m), BF16), v((m, 2 * face_n), BF16),
            v((m, loads + nm), BF16), v((m, loads + nm), BF16), v((m, loads), F32),
            v((m, loads), F32), v((m, loads), F32), v((m, loads), BF16), v((m, 3 * nm), BF16),
            v((2, face_n, nm), BF16), v((2 * face_n, loads + 2 * nm), BF16),
            v((subs * nm, subs * nm), BF16), v((3 * nm, loads), BF16),
            v((subs, nm, loads), BF16), v((subs, nm, loads), BF16), v((subs, nm, loads), BF16),
            v((subs, nm, 3 * nm), BF16), v((2, groups, nm, loads), BF16),
            v((2, groups - 1, nm, loads), BF16), v((nm, loads), BF16),
            v((2, nm, loads), BF16), v((2, nm, face_n), BF16), v((2, nm, face_n), BF16),
            v((2, 2, face_n, loads), BF16), v((2, 2, face_n, loads), BF16),
            v((2, face_n // 2, 2 * nm), BF16), v((2, face_n // 2, 2 * nm), BF16),
            dma((5,)), dma((m // ch,)), dma((m // ch,)),
            dma((4, subs - 1)), dma((4, subs - 1)), dma((2, groups - 1)), dma((2, groups - 1)),
            dma((2,)), dma((2,)), dma((2,)), dma((2,)), dma((2, 2)), dma((2, 2)),
            dma((2,)), dma((2,)),
        ],
        compiler_params=pltpu.CompilerParams(
            collective_id=0, has_side_effects=True, vmem_limit_bytes=60 * 1024 * 1024
        ),
    )(right_side, stiff_diag, dual_op, schur_op, jnp.swapaxes(modes, 1, 2), coarse, face_index)
    return pl.pallas_call(
        write_out,
        out_shape=(
            jax.ShapeDtypeStruct((1, m, loads), F32),
            jax.ShapeDtypeStruct((1, m, loads), BF16),
        ),
        in_specs=[pl.BlockSpec(memory_space=pltpu.VMEM)] * 2,
        out_specs=(any_spec, any_spec),
        scratch_shapes=[dma((2,))],
        compiler_params=pltpu.CompilerParams(vmem_limit_bytes=1024 * 1024),
    )(mult, res)


def solution(mesh):
    dims = (mesh.shape["sub"], mesh.shape["crow"], mesh.shape["ccol"])
    in_specs = (
        P(("sub", "crow", "ccol"), None, None),
        P(("sub", "crow", "ccol"), None),
        P(("sub", "crow", "ccol"), None, None),
        P(("sub", "crow", "ccol"), None, None),
        P(("sub", "crow", "ccol"), None, None),
        P(None, "sub", None, ("crow", "ccol"), None),
        P(),
    )
    out_specs = (P(("sub", "crow", "ccol"), None, None), P(("sub", "crow", "ccol"), None, None))
    return jax.shard_map(
        functools.partial(local, dims), mesh=mesh, in_specs=in_specs, out_specs=out_specs,
        check_vma=False,
    )
```

```python
import functools

import jax
import jax.numpy as jnp
from jax import lax
from jax.experimental import pallas as pl
from jax.experimental.pallas import tpu as pltpu
from jax.sharding import PartitionSpec as P

spectrum_low = 0.5
spectrum_high = 4.0
center = (spectrum_high + spectrum_low) / 2.0
half_width = (spectrum_high - spectrum_low) / 2.0
ratio_old = half_width / center
ratio_new = 1.0 / (2.0 * center / half_width - ratio_old)
carry = ratio_new * ratio_old
gain = 2.0 * ratio_new / half_width

F32 = jnp.float32
BF16 = jnp.bfloat16
MESH = pl.DeviceIdType.MESH


def mm(left, right):
    return jnp.dot(left, right, preferred_element_type=F32)


def kernel(
    dims,
    rhs_h, diag_h, dual_h, schur_h, modes_h, coarse_h, face_h,
    mult, res,
    rhs, diag, dual, schur, modes_t, modes, coarse, face,
    rows_of, pick, put, vec, work, base, step0, prod, own, gh, yz, cvec,
    ag, part, rs, solved, near, mf, mft, ysend, yrecv, zsend, zrecv,
    in_sem, sch_sem, dua_sem, ag_s, ag_r, rs_s, rs_r, nb_s, nb_r,
    hy_s, hy_r, hz_s, hz_r,
):
    subs, crows, ccols = dims
    groups = crows * ccols
    m = rhs.shape[0]
    loads = rhs.shape[1]
    nm = modes.shape[1]
    face_n = face.shape[1]
    ch = 512 if m % 512 == 0 else m
    chunks = m // ch
    half = face_n // 2
    inv = 1.0 / center
    sub = lax.axis_index("sub")
    crow = lax.axis_index("crow")
    ccol = lax.axis_index("ccol")
    group = crow * ccols + ccol
    flat = sub * groups + group

    def local(src, dst, sem):
        return pltpu.make_async_copy(src, dst, sem)

    loads_in = [
        local(rhs_h.at[0], rhs, in_sem.at[0]),
        local(modes_h.at[0], modes_t, in_sem.at[1]),
        local(face_h.at[flat], face, in_sem.at[2]),
        local(diag_h, diag, in_sem.at[3]),
        local(coarse_h, coarse, in_sem.at[4]),
    ]
    sch_in = [
        local(schur_h.at[0, pl.ds(k * ch, ch)], schur.at[pl.ds(k * ch, ch)], sch_sem.at[k])
        for k in range(chunks)
    ]
    dua_in = [
        local(dual_h.at[0, pl.ds(k * ch, ch)], dual.at[pl.ds(k * ch, ch)], dua_sem.at[k])
        for k in range(chunks)
    ]
    for c in loads_in[:3] + sch_in + loads_in[3:]:
        c.start()

    def sub_id(s):
        return (s, crow, ccol)

    def group_id(g):
        return (sub, g // ccols, lax.rem(g, ccols))

    barrier = pltpu.get_barrier_semaphore()
    for d in range(1, subs):
        pl.semaphore_signal(
            barrier, inc=1, device_id=sub_id(lax.rem(sub + d, subs)), device_id_type=MESH
        )
    for d in range(1, groups):
        pl.semaphore_signal(
            barrier, inc=1, device_id=group_id(lax.rem(group + d, groups)), device_id_type=MESH
        )

    def remote(src, dst, s_sem, r_sem, dev):
        return pltpu.make_async_remote_copy(
            src_ref=src, dst_ref=dst, send_sem=s_sem, recv_sem=r_sem,
            device_id=dev, device_id_type=MESH,
        )

    gathers = [
        [
            remote(ag.at[t, sub], ag.at[t, sub], ag_s.at[t, d - 1], ag_r.at[t, d - 1],
                   sub_id(lax.rem(sub + d, subs)))
            for d in range(1, subs)
        ]
        for t in range(2)
    ]
    far = [ccols // 2] + [c for c in range(1, ccols) if c != ccols // 2]
    hops = [(r, c) for r in range(1, crows) for c in far + [0]] + [(0, c) for c in far]
    scatters = []
    for t in range(2):
        row = []
        for d, (dr, dc) in enumerate(hops):
            r, c = lax.rem(crow + dr, crows), lax.rem(ccol + dc, ccols)
            row.append(
                remote(part.at[t, r * ccols + c], rs.at[t, d], rs_s.at[t, d], rs_r.at[t, d],
                       (sub, r, c))
            )
        scatters.append(row)
    has_next = sub < subs - 1
    has_prev = sub > 0
    after = sub_id(jnp.minimum(sub + 1, subs - 1))
    before = sub_id(jnp.maximum(sub - 1, 0))
    ends = ((0, 1, after, has_next, has_prev), (1, 0, before, has_prev, has_next))

    def near_copy(t, e):
        return remote(solved.at[t], near.at[t, e], nb_s.at[t, e], nb_r.at[t, e], ends[e][2])

    def y_copy(t, e):
        return remote(ysend.at[t, ends[e][1]], yrecv.at[t, e], hy_s.at[t, e], hy_r.at[t, e],
                      ends[e][2])

    def z_copy(e):
        return remote(zsend.at[ends[e][1]], zrecv.at[e], hz_s.at[e], hz_r.at[e], ends[e][2])

    def send(make):
        for e in range(2):
            pl.when(ends[e][3])(lambda e=e: make(e).start())

    def arrive(make):
        for e in range(2):
            pl.when(ends[e][4])(lambda e=e: make(e).wait_recv())

    def drain(make):
        for e in range(2):
            pl.when(ends[e][3])(lambda e=e: make(e).wait_send())

    for e in range(2):

        @pl.when(jnp.logical_not(ends[e][4]))
        def _(e=e):
            zrecv[e] = jnp.zeros_like(zrecv[e])
            for t in range(2):
                near[t, e] = jnp.zeros_like(near[t, e])
                yrecv[t, e] = jnp.zeros_like(yrecv[t, e])

    def rows(k):
        return pl.ds(k * ch, ch)

    loads_in[0].wait()
    loads_in[1].wait()
    ag[0, sub] = mm(modes_t[...], rhs[...]).astype(BF16)
    pl.semaphore_wait(barrier, subs - 1 + groups - 1)
    for c in gathers[0]:
        c.start()

    loads_in[2].wait()
    lane = lax.broadcasted_iota(jnp.int32, (face_n, 128), 1)
    for e in range(2):
        wide = jnp.broadcast_to(face[e:e + 1, :], (128, face_n)).T
        for c in range(m // 128):
            pick[e * face_n:(e + 1) * face_n, c * 128:(c + 1) * 128] = jnp.where(
                wide == lane + c * 128, 1.0, 0.0
            ).astype(BF16)
    modes[...] = modes_t[...].T
    vec[:, loads:loads + nm] = modes[...]
    work[:, loads + nm:] = modes[...]

    for k in range(chunks):
        sch_in[k].wait()
        dua_in[k].start()
    for k in range(chunks):
        u = mm(schur[rows(k), :], rhs[...]) * inv
        step0[rows(k), :] = u
        vec[rows(k), :loads] = u.astype(BF16)

    def scatter(t):
        for c in gathers[t]:
            c.wait_recv()
        part[t] = mm(coarse[...], ag[t].reshape(subs * nm, loads)).astype(BF16).reshape(groups, nm, loads)
        for c in scatters[t]:
            c.start()

    def total(t):
        out = part[t, group].astype(F32)
        for d in range(1, groups):
            scatters[t][d - 1].wait_recv()
            out = out + rs[t, d - 1].astype(F32)
        return out.astype(BF16)

    for c in dua_in:
        c.wait()
    for k in range(chunks):
        y = mm(dual[rows(k), :], vec[...])
        prod[rows(k), :] = y[:, :loads]
        work[rows(k), :loads + nm] = y.astype(BF16)
    for e in range(2):
        got = mm(pick[e * face_n:(e + 1) * face_n, :], work[...])
        ysend[0, e] = got[:, :loads].astype(BF16)
        faces = got[:, loads:loads + nm].astype(BF16)
        zsend[e] = jnp.concatenate([faces[:half], faces[half:]], axis=1)
        mf[e] = got[:, loads + nm:].astype(BF16)
    send(functools.partial(y_copy, 0))
    send(z_copy)
    loads_in[4].wait()
    scatter(0)

    loads_in[3].wait()
    sub_row = lax.broadcasted_iota(jnp.int32, (128, face_n), 0)
    for c in range(m // 128):
        span = slice(c * 128, (c + 1) * 128)
        for e in range(2):
            put[span, e * face_n:(e + 1) * face_n] = jnp.where(
                face[e:e + 1, :] == sub_row + c * 128, 1.0, 0.0
            ).astype(BF16)
        rows_of[span, :] = jnp.broadcast_to(diag[:, span], (128, 128)).T

    for e in range(2):
        mft[e] = mf[e].T
    for k in range(chunks):
        b = rhs[rows(k), :].astype(F32) - rows_of[rows(k), :] * step0[rows(k), :] - prod[rows(k), :]
        base[rows(k), :] = b
        own[rows(k), :] = b.astype(BF16)
        gh[rows(k), 2 * nm:] = (
            rows_of[rows(k), :nm] * modes[rows(k), :].astype(F32)
            + work[rows(k), loads:loads + nm].astype(F32)
        ).astype(BF16)
    plain = mm(modes_t[...], own[...])
    tie = mm(modes_t[...], gh[:, 2 * nm:]) * -inv
    solved[0] = total(0)
    send(functools.partial(near_copy, 0))
    for k in range(chunks):
        step0[rows(k), :] += mm(modes[rows(k), :], solved[0]) * inv
    arrive(functools.partial(y_copy, 0))
    plain = plain + mm(mft[0], yrecv[0, 0]) + mm(mft[1], yrecv[0, 1])
    arrive(z_copy)
    blank = jnp.zeros((face_n, nm), BF16)
    for e in range(2):
        span = slice(e * face_n, (e + 1) * face_n)
        yz[span, :loads] = yrecv[0, e]
        z = jnp.concatenate([zrecv[e, :, :nm], zrecv[e, :, nm:]], axis=0)
        yz[span, loads:] = jnp.concatenate([z, blank] if e == 0 else [blank, z], axis=1)
    ties = jnp.concatenate(
        [mm(mft[e], yz[e * face_n:(e + 1) * face_n, loads + e * nm:loads + (e + 1) * nm]) * inv
         for e in range(2)] + [tie],
        axis=1,
    ).astype(BF16)
    arrive(functools.partial(near_copy, 0))
    cvec[:2 * nm] = near[0].reshape(2 * nm, loads)
    cvec[2 * nm:] = solved[0]
    ag[1, sub] = (plain + mm(ties, cvec[...])).astype(BF16)
    for c in gathers[1]:
        c.start()
    cvec[2 * nm:] = -solved[0]
    for k in range(chunks):
        got = mm(put[rows(k), :], yz[...])
        base[rows(k), :] += got[:, :loads]
        gh[rows(k), :2 * nm] = got[:, loads:].astype(BF16)
    for k in range(chunks):
        r1 = base[rows(k), :] + mm(gh[rows(k), :], cvec[...]) * inv
        base[rows(k), :] = r1
        own[rows(k), :] = r1.astype(BF16)
    for k in range(chunks):
        w = carry * step0[rows(k), :] + gain * mm(schur[rows(k), :], own[...])
        prod[rows(k), :] = w
        vec[rows(k), :loads] = w.astype(BF16)

    scatter(1)
    for k in range(chunks):
        y = mm(dual[rows(k), :], vec[:, :loads])
        base[rows(k), :] = base[rows(k), :] - y - rows_of[rows(k), :] * prod[rows(k), :]
        own[rows(k), :] = y.astype(BF16)
    for e in range(2):
        ysend[1, e] = mm(pick[e * face_n:(e + 1) * face_n, :], own[...]).astype(BF16)
    send(functools.partial(y_copy, 1))

    solved[1] = total(1)
    send(functools.partial(near_copy, 1))
    for k in range(chunks):
        mult[rows(k), :] = (
            step0[rows(k), :] + prod[rows(k), :] + gain * mm(modes[rows(k), :], solved[1])
        )
        base[rows(k), :] -= gain * mm(gh[rows(k), 2 * nm:], solved[1])
    arrive(functools.partial(y_copy, 1))
    for k in range(chunks):
        base[rows(k), :] += mm(put[rows(k), :], yrecv[1].reshape(2 * face_n, loads))
    arrive(functools.partial(near_copy, 1))
    for k in range(chunks):
        res[rows(k), :] = (
            base[rows(k), :]
            + gain * mm(gh[rows(k), :2 * nm], near[1].reshape(2 * nm, loads))
        ).astype(BF16)
    for t in range(2):
        for c in gathers[t] + scatters[t]:
            c.wait_send()
        drain(functools.partial(y_copy, t))
        drain(functools.partial(near_copy, t))
    drain(z_copy)


def write_out(mult, res, mult_h, res_h, sem):
    copies = [
        pltpu.make_async_copy(mult, mult_h.at[0], sem.at[0]),
        pltpu.make_async_copy(res, res_h.at[0], sem.at[1]),
    ]
    for c in copies:
        c.start()
    for c in copies:
        c.wait()


def local(dims, right_side, stiff_diag, dual_op, schur_op, modes, coarse_inverse, face_index):
    subs, crows, ccols = dims
    groups = crows * ccols
    _, m, loads = right_side.shape
    nm = modes.shape[2]
    face_n = face_index.shape[2]
    coarse = coarse_inverse.reshape(
        coarse_inverse.shape[0] * coarse_inverse.shape[2], coarse_inverse.shape[4]
    )
    ch = 512 if m % 512 == 0 else m
    v = pltpu.VMEM
    dma = pltpu.SemaphoreType.DMA
    any_spec = pl.BlockSpec(memory_space=pl.ANY)
    mult, res = pl.pallas_call(
        functools.partial(kernel, dims),
        out_shape=(v((m, loads), F32), v((m, loads), BF16)),
        in_specs=[pl.BlockSpec(memory_space=pltpu.HBM)] * 7,
        out_specs=(pl.BlockSpec(memory_space=pltpu.VMEM),) * 2,
        scratch_shapes=[
            v((m, loads), BF16), v((1, m), F32), v((m, m), BF16), v((m, m), BF16),
            v((nm, m), BF16), v((m, nm), BF16), v(coarse.shape, BF16), v((2, face_n), jnp.int32),
            v((m, loads), F32), v((2 * face_n, m), BF16), v((m, 2 * face_n), BF16),
            v((m, loads + nm), BF16), v((m, loads + 2 * nm), BF16), v((m, loads), F32),
            v((m, loads), F32), v((m, loads), F32), v((m, loads), BF16), v((m, 3 * nm), BF16),
            v((2 * face_n, loads + 2 * nm), BF16), v((3 * nm, loads), BF16),
            v((2, subs, nm, loads), BF16), v((2, groups, nm, loads), BF16),
            v((2, groups - 1, nm, loads), BF16), v((2, nm, loads), BF16),
            v((2, 2, nm, loads), BF16), v((2, face_n, nm), BF16), v((2, nm, face_n), BF16),
            v((2, 2, face_n, loads), BF16), v((2, 2, face_n, loads), BF16),
            v((2, face_n // 2, 2 * nm), BF16), v((2, face_n // 2, 2 * nm), BF16),
            dma((5,)), dma((m // ch,)), dma((m // ch,)),
            dma((2, subs - 1)), dma((2, subs - 1)), dma((2, groups - 1)), dma((2, groups - 1)),
            dma((2, 2)), dma((2, 2)), dma((2, 2)), dma((2, 2)), dma((2,)), dma((2,)),
        ],
        compiler_params=pltpu.CompilerParams(
            collective_id=0, has_side_effects=True, vmem_limit_bytes=60 * 1024 * 1024
        ),
    )(right_side, stiff_diag, dual_op, schur_op, jnp.swapaxes(modes, 1, 2), coarse, face_index)
    return pl.pallas_call(
        write_out,
        out_shape=(
            jax.ShapeDtypeStruct((1, m, loads), F32),
            jax.ShapeDtypeStruct((1, m, loads), BF16),
        ),
        in_specs=[pl.BlockSpec(memory_space=pltpu.VMEM)] * 2,
        out_specs=(any_spec, any_spec),
        scratch_shapes=[dma((2,))],
        compiler_params=pltpu.CompilerParams(vmem_limit_bytes=1024 * 1024),
    )(mult, res)


def solution(mesh):
    dims = (mesh.shape["sub"], mesh.shape["crow"], mesh.shape["ccol"])
    in_specs = (
        P(("sub", "crow", "ccol"), None, None),
        P(("sub", "crow", "ccol"), None),
        P(("sub", "crow", "ccol"), None, None),
        P(("sub", "crow", "ccol"), None, None),
        P(("sub", "crow", "ccol"), None, None),
        P(None, "sub", None, ("crow", "ccol"), None),
        P(),
    )
    out_specs = (P(("sub", "crow", "ccol"), None, None), P(("sub", "crow", "ccol"), None, None))
    return jax.shard_map(
        functools.partial(local, dims), mesh=mesh, in_specs=in_specs, out_specs=out_specs,
        check_vma=False,
    )
```

```python
import functools

import jax
import jax.numpy as jnp
from jax import lax
from jax.experimental import pallas as pl
from jax.experimental.pallas import tpu as pltpu
from jax.sharding import PartitionSpec as P

spectrum_low = 0.5
spectrum_high = 4.0
center = (spectrum_high + spectrum_low) / 2.0
half_width = (spectrum_high - spectrum_low) / 2.0
ratio_old = half_width / center
ratio_new = 1.0 / (2.0 * center / half_width - ratio_old)
carry = ratio_new * ratio_old
gain = 2.0 * ratio_new / half_width

F32 = jnp.float32
BF16 = jnp.bfloat16
MESH = pl.DeviceIdType.MESH


def mm(left, right):
    return jnp.dot(left, right, preferred_element_type=F32)


def kernel(
    dims,
    rhs_h, diag_h, dual_h, schur_h, modes_h, coarse_h, face_h,
    mult, res,
    rhs, diag, dual, schur, modes_t, modes, coarse, face,
    rows_of, pick, put, vec, work, base, step0, prod, own, gh, yz, cvec,
    ag, part, rs, solved, near, mf, mft, ysend, yrecv, zsend, zrecv,
    in_sem, sch_sem, dua_sem, ag_s, ag_r, rs_s, rs_r, nb_s, nb_r,
    hy_s, hy_r, hz_s, hz_r,
):
    subs, crows, ccols = dims
    groups = crows * ccols
    m = rhs.shape[0]
    loads = rhs.shape[1]
    nm = modes.shape[1]
    face_n = face.shape[1]
    ch = 512 if m % 512 == 0 else m
    chunks = m // ch
    half = face_n // 2
    inv = 1.0 / center
    sub = lax.axis_index("sub")
    crow = lax.axis_index("crow")
    ccol = lax.axis_index("ccol")
    group = crow * ccols + ccol
    flat = sub * groups + group

    def local(src, dst, sem):
        return pltpu.make_async_copy(src, dst, sem)

    loads_in = [
        local(rhs_h.at[0], rhs, in_sem.at[0]),
        local(modes_h.at[0], modes_t, in_sem.at[1]),
        local(face_h.at[flat], face, in_sem.at[2]),
        local(diag_h, diag, in_sem.at[3]),
        local(coarse_h, coarse, in_sem.at[4]),
    ]
    sch_in = [
        local(schur_h.at[0, pl.ds(k * ch, ch)], schur.at[pl.ds(k * ch, ch)], sch_sem.at[k])
        for k in range(chunks)
    ]
    dua_in = [
        local(dual_h.at[0, pl.ds(k * ch, ch)], dual.at[pl.ds(k * ch, ch)], dua_sem.at[k])
        for k in range(chunks)
    ]
    for c in loads_in[:3] + sch_in + loads_in[3:]:
        c.start()

    def sub_id(s):
        return (s, crow, ccol)

    def group_id(g):
        return (sub, g // ccols, lax.rem(g, ccols))

    barrier = pltpu.get_barrier_semaphore()
    for d in range(1, subs):
        pl.semaphore_signal(
            barrier, inc=1, device_id=sub_id(lax.rem(sub + d, subs)), device_id_type=MESH
        )
    for d in range(1, groups):
        pl.semaphore_signal(
            barrier, inc=1, device_id=group_id(lax.rem(group + d, groups)), device_id_type=MESH
        )

    def remote(src, dst, s_sem, r_sem, dev):
        return pltpu.make_async_remote_copy(
            src_ref=src, dst_ref=dst, send_sem=s_sem, recv_sem=r_sem,
            device_id=dev, device_id_type=MESH,
        )

    gathers = [
        [
            remote(ag.at[t, sub], ag.at[t, sub], ag_s.at[t, d - 1], ag_r.at[t, d - 1],
                   sub_id(lax.rem(sub + d, subs)))
            for d in range(1, subs)
        ]
        for t in range(2)
    ]
    far = [ccols // 2] + [c for c in range(1, ccols) if c != ccols // 2]
    hops = [(r, c) for r in range(1, crows) for c in far + [0]] + [(0, c) for c in far]
    scatters = []
    for t in range(2):
        row = []
        for d, (dr, dc) in enumerate(hops):
            r, c = lax.rem(crow + dr, crows), lax.rem(ccol + dc, ccols)
            row.append(
                remote(part.at[t, r * ccols + c], rs.at[t, d], rs_s.at[t, d], rs_r.at[t, d],
                       (sub, r, c))
            )
        scatters.append(row)
    has_next = sub < subs - 1
    has_prev = sub > 0
    after = sub_id(jnp.minimum(sub + 1, subs - 1))
    before = sub_id(jnp.maximum(sub - 1, 0))
    ends = ((0, 1, after, has_next, has_prev), (1, 0, before, has_prev, has_next))

    def near_copy(t, e):
        return remote(solved.at[t], near.at[t, e], nb_s.at[t, e], nb_r.at[t, e], ends[e][2])

    def y_copy(t, e):
        return remote(ysend.at[t, ends[e][1]], yrecv.at[t, e], hy_s.at[t, e], hy_r.at[t, e],
                      ends[e][2])

    def z_copy(e):
        return remote(zsend.at[ends[e][1]], zrecv.at[e], hz_s.at[e], hz_r.at[e], ends[e][2])

    def send(make):
        for e in range(2):
            pl.when(ends[e][3])(lambda e=e: make(e).start())

    def arrive(make):
        for e in range(2):
            pl.when(ends[e][4])(lambda e=e: make(e).wait_recv())

    def drain(make):
        for e in range(2):
            pl.when(ends[e][3])(lambda e=e: make(e).wait_send())

    for e in range(2):

        @pl.when(jnp.logical_not(ends[e][4]))
        def _(e=e):
            zrecv[e] = jnp.zeros_like(zrecv[e])
            for t in range(2):
                near[t, e] = jnp.zeros_like(near[t, e])
                yrecv[t, e] = jnp.zeros_like(yrecv[t, e])

    def rows(k):
        return pl.ds(k * ch, ch)

    loads_in[0].wait()
    loads_in[1].wait()
    ag[0, sub] = mm(modes_t[...], rhs[...]).astype(BF16)
    pl.semaphore_wait(barrier, subs - 1 + groups - 1)
    for c in gathers[0]:
        c.start()

    loads_in[2].wait()
    lane = lax.broadcasted_iota(jnp.int32, (face_n, 128), 1)
    for e in range(2):
        wide = jnp.broadcast_to(face[e:e + 1, :], (128, face_n)).T
        for c in range(m // 128):
            pick[e * face_n:(e + 1) * face_n, c * 128:(c + 1) * 128] = jnp.where(
                wide == lane + c * 128, 1.0, 0.0
            ).astype(BF16)
    modes[...] = modes_t[...].T
    vec[:, loads:loads + nm] = modes[...]
    work[:, loads + nm:] = modes[...]

    for k in range(chunks):
        sch_in[k].wait()
        dua_in[k].start()
    for k in range(chunks):
        u = mm(schur[rows(k), :], rhs[...]) * inv
        step0[rows(k), :] = u
        vec[rows(k), :loads] = u.astype(BF16)

    def scatter(t):
        for c in gathers[t]:
            c.wait_recv()
        part[t] = mm(coarse[...], ag[t].reshape(subs * nm, loads)).astype(BF16).reshape(groups, nm, loads)
        for c in scatters[t]:
            c.start()

    def total(t):
        out = part[t, group].astype(F32)
        for d in range(1, groups):
            scatters[t][d - 1].wait_recv()
            out = out + rs[t, d - 1].astype(F32)
        return out.astype(BF16)

    loads_in[4].wait()
    scatter(0)

    for c in dua_in:
        c.wait()
    for k in range(chunks):
        y = mm(dual[rows(k), :], vec[...])
        prod[rows(k), :] = y[:, :loads]
        work[rows(k), :loads + nm] = y.astype(BF16)
    for e in range(2):
        got = mm(pick[e * face_n:(e + 1) * face_n, :], work[...])
        ysend[0, e] = got[:, :loads].astype(BF16)
        faces = got[:, loads:loads + nm].astype(BF16)
        zsend[e] = jnp.concatenate([faces[:half], faces[half:]], axis=1)
        mf[e] = got[:, loads + nm:].astype(BF16)
    send(functools.partial(y_copy, 0))
    send(z_copy)
    loads_in[3].wait()
    sub_row = lax.broadcasted_iota(jnp.int32, (128, face_n), 0)
    for c in range(m // 128):
        span = slice(c * 128, (c + 1) * 128)
        for e in range(2):
            put[span, e * face_n:(e + 1) * face_n] = jnp.where(
                face[e:e + 1, :] == sub_row + c * 128, 1.0, 0.0
            ).astype(BF16)
        rows_of[span, :] = jnp.broadcast_to(diag[:, span], (128, 128)).T

    solved[0] = total(0)
    send(functools.partial(near_copy, 0))
    for e in range(2):
        mft[e] = mf[e].T
    for k in range(chunks):
        b = rhs[rows(k), :].astype(F32) - rows_of[rows(k), :] * step0[rows(k), :] - prod[rows(k), :]
        base[rows(k), :] = b
        own[rows(k), :] = b.astype(BF16)
        gh[rows(k), 2 * nm:] = (
            rows_of[rows(k), :nm] * modes[rows(k), :].astype(F32)
            + work[rows(k), loads:loads + nm].astype(F32)
        ).astype(BF16)
    plain = mm(modes_t[...], own[...])
    tie = mm(modes_t[...], gh[:, 2 * nm:]) * -inv
    for k in range(chunks):
        step0[rows(k), :] += mm(modes[rows(k), :], solved[0]) * inv
    arrive(functools.partial(y_copy, 0))
    plain = plain + mm(mft[0], yrecv[0, 0]) + mm(mft[1], yrecv[0, 1])
    arrive(z_copy)
    blank = jnp.zeros((face_n, nm), BF16)
    for e in range(2):
        span = slice(e * face_n, (e + 1) * face_n)
        yz[span, :loads] = yrecv[0, e]
        z = jnp.concatenate([zrecv[e, :, :nm], zrecv[e, :, nm:]], axis=0)
        yz[span, loads:] = jnp.concatenate([z, blank] if e == 0 else [blank, z], axis=1)
    ties = jnp.concatenate(
        [mm(mft[e], yz[e * face_n:(e + 1) * face_n, loads + e * nm:loads + (e + 1) * nm]) * inv
         for e in range(2)] + [tie],
        axis=1,
    ).astype(BF16)
    arrive(functools.partial(near_copy, 0))
    cvec[:2 * nm] = near[0].reshape(2 * nm, loads)
    cvec[2 * nm:] = solved[0]
    ag[1, sub] = (plain + mm(ties, cvec[...])).astype(BF16)
    for c in gathers[1]:
        c.start()
    cvec[2 * nm:] = -solved[0]
    for k in range(chunks):
        got = mm(put[rows(k), :], yz[...])
        base[rows(k), :] += got[:, :loads]
        gh[rows(k), :2 * nm] = got[:, loads:].astype(BF16)
    for k in range(chunks):
        r1 = base[rows(k), :] + mm(gh[rows(k), :], cvec[...]) * inv
        base[rows(k), :] = r1
        own[rows(k), :] = r1.astype(BF16)
    for k in range(chunks):
        w = carry * step0[rows(k), :] + gain * mm(schur[rows(k), :], own[...])
        prod[rows(k), :] = w
        vec[rows(k), :loads] = w.astype(BF16)

    scatter(1)
    for k in range(chunks):
        y = mm(dual[rows(k), :], vec[:, :loads])
        base[rows(k), :] = base[rows(k), :] - y - rows_of[rows(k), :] * prod[rows(k), :]
        own[rows(k), :] = y.astype(BF16)
    for e in range(2):
        ysend[1, e] = mm(pick[e * face_n:(e + 1) * face_n, :], own[...]).astype(BF16)
    send(functools.partial(y_copy, 1))

    solved[1] = total(1)
    send(functools.partial(near_copy, 1))
    for k in range(chunks):
        mult[rows(k), :] = (
            step0[rows(k), :] + prod[rows(k), :] + gain * mm(modes[rows(k), :], solved[1])
        )
        base[rows(k), :] -= gain * mm(gh[rows(k), 2 * nm:], solved[1])
    arrive(functools.partial(y_copy, 1))
    for k in range(chunks):
        base[rows(k), :] += mm(put[rows(k), :], yrecv[1].reshape(2 * face_n, loads))
    arrive(functools.partial(near_copy, 1))
    for k in range(chunks):
        res[rows(k), :] = (
            base[rows(k), :]
            + gain * mm(gh[rows(k), :2 * nm], near[1].reshape(2 * nm, loads))
        ).astype(BF16)
    for t in range(2):
        for c in gathers[t] + scatters[t]:
            c.wait_send()
        drain(functools.partial(y_copy, t))
        drain(functools.partial(near_copy, t))
    drain(z_copy)


def write_out(mult, res, mult_h, res_h, sem):
    copies = [
        pltpu.make_async_copy(mult, mult_h.at[0], sem.at[0]),
        pltpu.make_async_copy(res, res_h.at[0], sem.at[1]),
    ]
    for c in copies:
        c.start()
    for c in copies:
        c.wait()


def local(dims, right_side, stiff_diag, dual_op, schur_op, modes, coarse_inverse, face_index):
    subs, crows, ccols = dims
    groups = crows * ccols
    _, m, loads = right_side.shape
    nm = modes.shape[2]
    face_n = face_index.shape[2]
    coarse = coarse_inverse.reshape(
        coarse_inverse.shape[0] * coarse_inverse.shape[2], coarse_inverse.shape[4]
    )
    ch = 512 if m % 512 == 0 else m
    v = pltpu.VMEM
    dma = pltpu.SemaphoreType.DMA
    any_spec = pl.BlockSpec(memory_space=pl.ANY)
    mult, res = pl.pallas_call(
        functools.partial(kernel, dims),
        out_shape=(v((m, loads), F32), v((m, loads), BF16)),
        in_specs=[pl.BlockSpec(memory_space=pltpu.HBM)] * 7,
        out_specs=(pl.BlockSpec(memory_space=pltpu.VMEM),) * 2,
        scratch_shapes=[
            v((m, loads), BF16), v((1, m), F32), v((m, m), BF16), v((m, m), BF16),
            v((nm, m), BF16), v((m, nm), BF16), v(coarse.shape, BF16), v((2, face_n), jnp.int32),
            v((m, loads), F32), v((2 * face_n, m), BF16), v((m, 2 * face_n), BF16),
            v((m, loads + nm), BF16), v((m, loads + 2 * nm), BF16), v((m, loads), F32),
            v((m, loads), F32), v((m, loads), F32), v((m, loads), BF16), v((m, 3 * nm), BF16),
            v((2 * face_n, loads + 2 * nm), BF16), v((3 * nm, loads), BF16),
            v((2, subs, nm, loads), BF16), v((2, groups, nm, loads), BF16),
            v((2, groups - 1, nm, loads), BF16), v((2, nm, loads), BF16),
            v((2, 2, nm, loads), BF16), v((2, face_n, nm), BF16), v((2, nm, face_n), BF16),
            v((2, 2, face_n, loads), BF16), v((2, 2, face_n, loads), BF16),
            v((2, face_n // 2, 2 * nm), BF16), v((2, face_n // 2, 2 * nm), BF16),
            dma((5,)), dma((m // ch,)), dma((m // ch,)),
            dma((2, subs - 1)), dma((2, subs - 1)), dma((2, groups - 1)), dma((2, groups - 1)),
            dma((2, 2)), dma((2, 2)), dma((2, 2)), dma((2, 2)), dma((2,)), dma((2,)),
        ],
        compiler_params=pltpu.CompilerParams(
            collective_id=0, has_side_effects=True, vmem_limit_bytes=60 * 1024 * 1024
        ),
    )(right_side, stiff_diag, dual_op, schur_op, jnp.swapaxes(modes, 1, 2), coarse, face_index)
    return pl.pallas_call(
        write_out,
        out_shape=(
            jax.ShapeDtypeStruct((1, m, loads), F32),
            jax.ShapeDtypeStruct((1, m, loads), BF16),
        ),
        in_specs=[pl.BlockSpec(memory_space=pltpu.VMEM)] * 2,
        out_specs=(any_spec, any_spec),
        scratch_shapes=[dma((2,))],
        compiler_params=pltpu.CompilerParams(vmem_limit_bytes=1024 * 1024),
    )(mult, res)


def solution(mesh):
    dims = (mesh.shape["sub"], mesh.shape["crow"], mesh.shape["ccol"])
    in_specs = (
        P(("sub", "crow", "ccol"), None, None),
        P(("sub", "crow", "ccol"), None),
        P(("sub", "crow", "ccol"), None, None),
        P(("sub", "crow", "ccol"), None, None),
        P(("sub", "crow", "ccol"), None, None),
        P(None, "sub", None, ("crow", "ccol"), None),
        P(),
    )
    out_specs = (P(("sub", "crow", "ccol"), None, None), P(("sub", "crow", "ccol"), None, None))
    return jax.shard_map(
        functools.partial(local, dims), mesh=mesh, in_specs=in_specs, out_specs=out_specs,
        check_vma=False,
    )
```
